512 devices in a mesh: cell: 32 (over z_lo, x, core), feat: 16 (over z_hi, y).
Axes of the slice: x: 4, y: 4, z: 16 (z_hi: 4, z_lo: 4; z = z_hi * 4 + z_lo), core: 2. Of those that a mesh axis runs over, the one named last changes fastest.
Arguments:
- rna_counts: bfloat16 [65536, 4096], P('cell', 'feat'), may hold values from -6 to 6
- rna_embed: bfloat16 [65536, 64], P('cell'), may hold values from -3 to 3
- rna_potential: float32 [65536], P('cell'), may hold values from -1 to 1
- atac_counts: bfloat16 [16384, 16384], P('feat', 'cell'), may hold values from -6 to 6
- atac_embed: bfloat16 [16384, 64], P('feat'), may hold values from -3 to 3
- atac_potential: bfloat16 [16384], P('feat'), may hold values from -1 to 1
- panel_ids: int32 [1024], P('feat'), may hold values from 0 to 16383, as said below
Outputs:
- feature_cross: bfloat16 [4096, 16384], P('feat', 'cell')
- gene_term: float32 [4096], P('feat')
- peak_term: float32 [16384], P('cell')
The draws below stay inside these ranges and needn't reach their ends.
Inputs may be any that keep to these rules, and one draw needn't show every extreme that they name: `panel_ids`: the ids in slots k * 64 to (k + 1) * 64 - 1 are distinct and lie among ATAC cells k * 1024 to (k + 1) * 1024 - 1.
All inputs are finite; a program needn't handle non-finite values.
Results may differ from the reference program's by a relative error of at most 0.0058.
Values may be sent and summed in bfloat16 or wider, within the bound.
A program may use at most 64 MiB of HBM per device.

```python
import math
import jax
import jax.numpy as jnp
from jax import lax

GENES = 4096
PEAKS = 16384
EMB = 64
PANEL = 1024
ATAC_DEV = 1024
RNA = 65536
ATAC_CELLS = 16384
PANEL_DEV = 64


def draw_owner_slots(single):
    first_key = jax.random.fold_in(single, 1)
    second_key = jax.random.fold_in(single, 2)
    inner = jax.random.permutation(first_key, ATAC_DEV - 2)[:PANEL_DEV - 2].astype(jnp.int32) + 1
    ends = jnp.array([0, ATAC_DEV - 1], dtype=jnp.int32)
    values = jnp.concatenate([ends, inner])
    shuffle = jax.random.permutation(second_key, PANEL_DEV).astype(jnp.int32)
    return jnp.take(values, shuffle, axis=0)


def draw_panel_ids(key, part):
    owners = ATAC_CELLS // ATAC_DEV
    keys = jax.random.split(key, owners)
    picked = jax.vmap(draw_owner_slots)(keys)
    base = (jnp.arange(owners, dtype=jnp.int32) * ATAC_DEV)[:, None]
    return (picked.astype(jnp.int32) + base).reshape(PANEL)


def block_levels(own_key, dims, cuts, low, top_value):
    factor_of = 1.0
    for dim, shards_of in cuts:
        draws = jax.random.uniform(jax.random.fold_in(jax.random.fold_in(own_key, 6), dim), (shards_of,), jnp.float32, low / len(cuts), top_value / len(cuts))
        factor_of = factor_of * jnp.repeat(jnp.exp(draws), dims[dim] // shards_of).reshape((-1,) + (1,) * (len(dims) - 1 - dim))
    return factor_of


def bell_draw(stream_key, extent, width, bound, cuts=(), held_as=jnp.bfloat16):
    drawn = jax.random.normal(stream_key, extent, jnp.float32) * width
    if len(cuts) > 0:
        drawn = block_levels(stream_key, extent, cuts, -0.22, 0.18) * drawn
    return jnp.clip(drawn, min=-bound, max=bound).astype(held_as)


def setup_inputs(seed: int = 0) -> dict:
    key_of = jax.random.split(jax.random.key(seed), 8)
    return {
        "rna_counts": bell_draw(key_of[0], (RNA, GENES), 1.0, 6.0, ((0, 32), (1, 16))),
        "rna_embed": bell_draw(key_of[1], (RNA, EMB), 1.0, 3.0, ((0, 32),)),
        "rna_potential": jnp.clip(jax.random.uniform(key_of[2], (RNA,), jnp.float32, -1.0, 1.0) * block_levels(key_of[2], (RNA,), ((0, 32),), -0.4, 0.0), -1.0, 1.0),
        "atac_counts": bell_draw(key_of[3], (ATAC_CELLS, PEAKS), 1.0, 6.0, ((0, 16), (1, 32))),
        "atac_embed": bell_draw(key_of[4], (ATAC_CELLS, EMB), 1.0, 3.0, ((0, 16),)),
        "atac_potential": jnp.clip(jax.random.uniform(key_of[5], (ATAC_CELLS,), jnp.float32, -1.0, 1.0) * block_levels(key_of[5], (ATAC_CELLS,), ((0, 16),), -0.4, 0.0), -1.0, 1.0).astype(jnp.bfloat16),
        "panel_ids": draw_panel_ids(jax.random.fold_in(key_of[7], 71), 0),
    }


def reference(rna_counts, rna_embed, rna_potential, atac_counts, atac_embed, atac_potential, panel_ids):
    panel_rows = jnp.take(atac_counts, panel_ids, axis=0)
    panel_embed = jnp.take(atac_embed, panel_ids, axis=0)
    panel_potential = jnp.take(atac_potential, panel_ids, axis=0).astype(jnp.float32)
    inverse = 1.0 / math.sqrt(EMB)
    height = min(4096, RNA)
    number = RNA // height
    items = (rna_counts.reshape(number, height, GENES), rna_embed.reshape(number, height, EMB), rna_potential.reshape(number, height))

    def advance(carry, item):
        total, gene_sum, panel_mass = carry
        block_rows, block_embed, block_potential = item
        score = lax.dot_general(block_embed, panel_embed, (((1,), (1,)), ((), ())), preferred_element_type=jnp.float32)
        coupling = jnp.exp(block_potential[:, None] + panel_potential[None, :] + score * inverse).astype(jnp.bfloat16)
        widened = coupling.astype(jnp.float32)
        row_mass = lax.optimization_barrier(jnp.sum(widened, axis=1))
        panel_mass = panel_mass + lax.optimization_barrier(jnp.sum(widened, axis=0))
        total = total + lax.dot_general(block_rows, coupling, (((0,), (0,)), ((), ())), preferred_element_type=jnp.float32)
        squares = jnp.square(block_rows.astype(jnp.float32))
        gene_sum = gene_sum + jnp.dot(row_mass, squares, precision=lax.Precision.HIGHEST)
        return ((total, gene_sum, panel_mass), None)
    start = (jnp.zeros((GENES, PANEL), jnp.float32), jnp.zeros((GENES,), jnp.float32), jnp.zeros((PANEL,), jnp.float32))
    (total, gene_sum, panel_mass), unused = lax.scan(advance, start, items)
    reduced = total.astype(jnp.bfloat16)
    scale = 1.0 / math.sqrt(RNA * PANEL)
    mass_scale = 1.0 / (RNA * PANEL)
    feature_cross = (jnp.dot(reduced, panel_rows, preferred_element_type=jnp.float32) * scale).astype(jnp.bfloat16)
    gene_term = gene_sum * mass_scale
    peak_term = jnp.dot(panel_mass, jnp.square(panel_rows.astype(jnp.float32)), precision=lax.Precision.HIGHEST) * mass_scale
    return (feature_cross, gene_term, peak_term)
```

```python
import math

import jax
import jax.numpy as jnp
from jax import lax
from jax.sharding import Mesh
from jax.sharding import PartitionSpec as P

CELL = ("z_lo", "x", "core")
FEAT = ("z_hi", "y")
SIZES = {"z_lo": 4, "x": 4, "core": 2, "z_hi": 4, "y": 4}
HALVING = (("core", 1), ("x", 1), ("z_lo", 1), ("x", 2), ("z_lo", 2))


def _half(piece, axis, bit):
    h = piece.shape[0] // 2
    upper = ((lax.axis_index(axis) & bit) != 0).astype(jnp.int32)
    keep = lax.dynamic_slice_in_dim(piece, upper * h, h, axis=0)
    send = lax.dynamic_slice_in_dim(piece, (1 - upper) * h, h, axis=0)
    return keep, send


def _swap(value, axis, bit):
    return lax.ppermute(value, axis, [(i, i ^ bit) for i in range(SIZES[axis])])


def _join(piece, got, axis, bit):
    lower = (lax.axis_index(axis) & bit) == 0
    return jnp.where(lower, jnp.concatenate([piece, got]), jnp.concatenate([got, piece]))


def cell_sum(total, masses):
    for axis, bit in HALVING:
        keep_t, send_t = _half(total, axis, bit)
        keep_m, send_m = _half(masses, axis, bit)
        got_t, got_m = _swap((send_t, send_m), axis, bit)
        total, masses = keep_t + got_t, keep_m + got_m
    reduced = total.astype(jnp.bfloat16)
    for axis, bit in reversed(HALVING):
        got_t, got_m = _swap((reduced, masses), axis, bit)
        reduced = _join(reduced, got_t, axis, bit)
        masses = _join(masses, got_m, axis, bit)
    return reduced, masses


def local(rna_counts, rna_embed, rna_potential, atac_counts, atac_embed, atac_potential, panel_ids):
    owner = lax.axis_index(FEAT)
    local_ids = panel_ids - owner * atac_counts.shape[0]
    chosen_rows = jnp.take(atac_counts, local_ids, axis=0)
    chosen_embed = jnp.take(atac_embed, local_ids, axis=0)
    chosen_potential = jnp.take(atac_potential, local_ids, axis=0)
    small = jnp.concatenate([chosen_embed, chosen_potential[:, None]], axis=1)
    small = lax.all_gather(small, "y", axis=0, tiled=True)
    small = lax.all_gather(small, "z_hi", axis=0, tiled=True)
    panel_embed = small[:, :-1]
    panel_float = small[:, -1].astype(jnp.float32)
    panel_rows = lax.all_gather(chosen_rows, FEAT, axis=0, tiled=True)
    inverse = 1.0 / math.sqrt(rna_embed.shape[1])
    rows_here = rna_counts.shape[0]
    genes_here = rna_counts.shape[1]
    panel_size = panel_embed.shape[0]
    height = min(512, rows_here)
    number = rows_here // height
    items = (
        rna_counts.reshape(number, height, genes_here),
        rna_embed.reshape(number, height, rna_embed.shape[1]),
        rna_potential.reshape(number, height),
    )

    def advance(carry, item):
        total, gene_sum, panel_mass = carry
        block_rows, block_embed, block_potential = item
        score = lax.dot_general(
            block_embed, panel_embed, (((1,), (1,)), ((), ())), preferred_element_type=jnp.float32
        )
        coupling = jnp.exp(
            block_potential[:, None] + panel_float[None, :] + score * inverse
        ).astype(jnp.bfloat16)
        widened = coupling.astype(jnp.float32)
        row_mass = jnp.sum(widened, axis=1)
        panel_mass = panel_mass + jnp.sum(widened, axis=0)
        total = total + lax.dot_general(
            block_rows, coupling, (((0,), (0,)), ((), ())), preferred_element_type=jnp.float32
        )
        squares = jnp.square(block_rows.astype(jnp.float32))
        gene_sum = gene_sum + jnp.dot(row_mass, squares, precision=lax.Precision.HIGHEST)
        return ((total, gene_sum, panel_mass), None)

    start = (
        jnp.zeros((genes_here, panel_size), jnp.float32),
        jnp.zeros((genes_here,), jnp.float32),
        jnp.zeros((panel_size,), jnp.float32),
    )
    (total, gene_sum, panel_mass), unused = lax.scan(advance, start, items)
    reduced, masses = cell_sum(total, jnp.concatenate([gene_sum, panel_mass]))
    gene_sum = masses[:genes_here]
    panel_mass = masses[genes_here:]
    all_rows = rows_here * lax.axis_size(CELL)
    scale = 1.0 / math.sqrt(all_rows * panel_size)
    mass_scale = 1.0 / (all_rows * panel_size)
    feature_cross = (
        jnp.dot(reduced, panel_rows, preferred_element_type=jnp.float32) * scale
    ).astype(jnp.bfloat16)
    gene_term = gene_sum * mass_scale
    peak_term = (
        jnp.dot(
            panel_mass, jnp.square(panel_rows.astype(jnp.float32)), precision=lax.Precision.HIGHEST
        )
        * mass_scale
    )
    return (feature_cross, gene_term, peak_term)


def solution(mesh):
    split = Mesh(mesh.devices.reshape(4, 4, 2, 4, 4), CELL + FEAT)
    placed = (
        P(CELL, FEAT),
        P(CELL, None),
        P(CELL),
        P(FEAT, CELL),
        P(FEAT, None),
        P(FEAT),
        P(FEAT),
    )
    return jax.shard_map(
        local,
        mesh=split,
        in_specs=placed,
        out_specs=(P(FEAT, CELL), P(FEAT), P(CELL)),
        check_vma=False,
    )
```

```python
import math

import jax
import jax.numpy as jnp
from jax import lax
from jax.sharding import Mesh
from jax.sharding import PartitionSpec as P

CELL = ("z_lo", "x", "core")
FEAT = ("z_hi", "y")
SIZES = {"z_lo": 4, "x": 4, "core": 2, "z_hi": 4, "y": 4}
HALVING = (("core", 1), ("x", 1), ("z_lo", 1), ("x", 2), ("z_lo", 2))


def _half(piece, axis, bit):
    h = piece.shape[0] // 2
    upper = ((lax.axis_index(axis) & bit) != 0).astype(jnp.int32)
    keep = lax.dynamic_slice_in_dim(piece, upper * h, h, axis=0)
    send = lax.dynamic_slice_in_dim(piece, (1 - upper) * h, h, axis=0)
    return keep, send


def _swap(value, axis, bit):
    return lax.ppermute(value, axis, [(i, i ^ bit) for i in range(SIZES[axis])])


def _join(piece, got, axis, bit):
    lower = (lax.axis_index(axis) & bit) == 0
    return jnp.where(lower, jnp.concatenate([piece, got]), jnp.concatenate([got, piece]))


def cell_sum(total, masses):
    parts = 2 ** len(HALVING)
    genes, panel = total.shape
    packed = jnp.concatenate(
        [total.reshape(parts, -1), masses.reshape(parts, -1)], axis=1
    )
    for axis, bit in HALVING:
        keep, send = _half(packed, axis, bit)
        packed = keep + _swap(send, axis, bit)
    for axis, bit in reversed(HALVING):
        packed = _join(packed, _swap(packed, axis, bit), axis, bit)
    cut = total.size // parts
    reduced = packed[:, :cut].reshape(genes, panel).astype(jnp.bfloat16)
    return reduced, packed[:, cut:].reshape(-1)


def local(rna_counts, rna_embed, rna_potential, atac_counts, atac_embed, atac_potential, panel_ids):
    owner = lax.axis_index(FEAT)
    local_ids = panel_ids - owner * atac_counts.shape[0]
    chosen_rows = jnp.take(atac_counts, local_ids, axis=0)
    chosen_embed = jnp.take(atac_embed, local_ids, axis=0)
    chosen_potential = jnp.take(atac_potential, local_ids, axis=0)
    width = chosen_rows.shape[1]
    panel = jnp.concatenate([chosen_rows, chosen_embed, chosen_potential[:, None]], axis=1)
    panel = lax.all_gather(panel, "y", axis=0, tiled=True)
    panel = lax.all_gather(panel, "z_hi", axis=0, tiled=True)
    panel_rows = panel[:, :width]
    panel_embed = panel[:, width:-1]
    panel_float = panel[:, -1].astype(jnp.float32)
    inverse = 1.0 / math.sqrt(rna_embed.shape[1])
    rows_here = rna_counts.shape[0]
    genes_here = rna_counts.shape[1]
    panel_size = panel_embed.shape[0]
    height = min(512, rows_here)
    number = rows_here // height
    items = (
        rna_counts.reshape(number, height, genes_here),
        rna_embed.reshape(number, height, rna_embed.shape[1]),
        rna_potential.reshape(number, height),
    )

    def advance(carry, item):
        total, gene_sum, panel_mass = carry
        block_rows, block_embed, block_potential = item
        score = lax.dot_general(
            block_embed, panel_embed, (((1,), (1,)), ((), ())), preferred_element_type=jnp.float32
        )
        coupling = jnp.exp(
            block_potential[:, None] + panel_float[None, :] + score * inverse
        ).astype(jnp.bfloat16)
        widened = coupling.astype(jnp.float32)
        row_mass = jnp.sum(widened, axis=1)
        panel_mass = panel_mass + jnp.sum(widened, axis=0)
        total = total + lax.dot_general(
            block_rows, coupling, (((0,), (0,)), ((), ())), preferred_element_type=jnp.float32
        )
        squares = jnp.square(block_rows.astype(jnp.float32))
        gene_sum = gene_sum + jnp.dot(row_mass, squares, precision=lax.Precision.HIGHEST)
        return ((total, gene_sum, panel_mass), None)

    start = (
        jnp.zeros((genes_here, panel_size), jnp.float32),
        jnp.zeros((genes_here,), jnp.float32),
        jnp.zeros((panel_size,), jnp.float32),
    )
    (total, gene_sum, panel_mass), unused = lax.scan(advance, start, items)
    reduced, masses = cell_sum(total, jnp.concatenate([gene_sum, panel_mass]))
    gene_sum = masses[:genes_here]
    panel_mass = masses[genes_here:]
    all_rows = rows_here * lax.axis_size(CELL)
    scale = 1.0 / math.sqrt(all_rows * panel_size)
    mass_scale = 1.0 / (all_rows * panel_size)
    feature_cross = (
        jnp.dot(reduced, panel_rows, preferred_element_type=jnp.float32) * scale
    ).astype(jnp.bfloat16)
    gene_term = gene_sum * mass_scale
    peak_term = (
        jnp.dot(
            panel_mass, jnp.square(panel_rows.astype(jnp.float32)), precision=lax.Precision.HIGHEST
        )
        * mass_scale
    )
    return (feature_cross, gene_term, peak_term)


def solution(mesh):
    split = Mesh(mesh.devices.reshape(4, 4, 2, 4, 4), CELL + FEAT)
    placed = (
        P(CELL, FEAT),
        P(CELL, None),
        P(CELL),
        P(FEAT, CELL),
        P(FEAT, None),
        P(FEAT),
        P(FEAT),
    )
    return jax.shard_map(
        local,
        mesh=split,
        in_specs=placed,
        out_specs=(P(FEAT, CELL), P(FEAT), P(CELL)),
        check_vma=False,
    )
```

```python
import math

import jax
import jax.numpy as jnp
from jax import lax
from jax.sharding import Mesh
from jax.sharding import PartitionSpec as P

CELL = ("z_lo", "x", "core")
FEAT = ("z_hi", "y")
SIZES = {"z_lo": 4, "x": 4, "core": 2, "z_hi": 4, "y": 4}
HALVING = (("core", 1), ("x", 1), ("z_lo", 1), ("x", 2), ("z_lo", 2))


def _half(piece, axis, bit):
    h = piece.shape[0] // 2
    upper = ((lax.axis_index(axis) & bit) != 0).astype(jnp.int32)
    keep = lax.dynamic_slice_in_dim(piece, upper * h, h, axis=0)
    send = lax.dynamic_slice_in_dim(piece, (1 - upper) * h, h, axis=0)
    return keep, send


def _swap(value, axis, bit):
    return lax.ppermute(value, axis, [(i, i ^ bit) for i in range(SIZES[axis])])


def _join(piece, got, axis, bit):
    lower = (lax.axis_index(axis) & bit) == 0
    return jnp.where(lower, jnp.concatenate([piece, got]), jnp.concatenate([got, piece]))


def cell_sum(total, masses):
    parts = 2 ** len(HALVING)
    genes, panel = total.shape
    packed = jnp.concatenate(
        [total.reshape(parts, -1), masses.reshape(parts, -1)], axis=1
    )
    for axis, bit in HALVING:
        keep, send = _half(packed, axis, bit)
        packed = keep + _swap(send, axis, bit)
    for axis, bit in reversed(HALVING):
        packed = _join(packed, _swap(packed, axis, bit), axis, bit)
    cut = total.size // parts
    reduced = packed[:, :cut].reshape(genes, panel).astype(jnp.bfloat16)
    return reduced, packed[:, cut:].reshape(-1)


def local(rna_counts, rna_embed, rna_potential, atac_counts, atac_embed, atac_potential, panel_ids):
    owner = lax.axis_index(FEAT)
    local_ids = panel_ids - owner * atac_counts.shape[0]
    chosen_rows = jnp.take(atac_counts, local_ids, axis=0)
    chosen_embed = jnp.take(atac_embed, local_ids, axis=0)
    chosen_potential = jnp.take(atac_potential, local_ids, axis=0)
    small = jnp.concatenate([chosen_embed, chosen_potential[:, None]], axis=1)
    small = lax.all_gather(small, "y", axis=0, tiled=True)
    small = lax.all_gather(small, "z_hi", axis=0, tiled=True)
    panel_embed = small[:, :-1]
    panel_float = small[:, -1].astype(jnp.float32)
    panel_rows = lax.all_gather(chosen_rows, FEAT, axis=0, tiled=True)
    inverse = 1.0 / math.sqrt(rna_embed.shape[1])
    rows_here = rna_counts.shape[0]
    genes_here = rna_counts.shape[1]
    panel_size = panel_embed.shape[0]
    height = min(512, rows_here)
    number = rows_here // height
    items = (
        rna_counts.reshape(number, height, genes_here),
        rna_embed.reshape(number, height, rna_embed.shape[1]),
        rna_potential.reshape(number, height),
    )

    def advance(carry, item):
        total, gene_sum, panel_mass = carry
        block_rows, block_embed, block_potential = item
        score = lax.dot_general(
            block_embed, panel_embed, (((1,), (1,)), ((), ())), preferred_element_type=jnp.float32
        )
        coupling = jnp.exp(
            block_potential[:, None] + panel_float[None, :] + score * inverse
        ).astype(jnp.bfloat16)
        widened = coupling.astype(jnp.float32)
        row_mass = jnp.sum(widened, axis=1)
        panel_mass = panel_mass + jnp.sum(widened, axis=0)
        total = total + lax.dot_general(
            block_rows, coupling, (((0,), (0,)), ((), ())), preferred_element_type=jnp.float32
        )
        squares = jnp.square(block_rows.astype(jnp.float32))
        gene_sum = gene_sum + jnp.dot(row_mass, squares, precision=lax.Precision.HIGHEST)
        return ((total, gene_sum, panel_mass), None)

    start = (
        jnp.zeros((genes_here, panel_size), jnp.float32),
        jnp.zeros((genes_here,), jnp.float32),
        jnp.zeros((panel_size,), jnp.float32),
    )
    (total, gene_sum, panel_mass), unused = lax.scan(advance, start, items)
    reduced, masses = cell_sum(total, jnp.concatenate([gene_sum, panel_mass]))
    gene_sum = masses[:genes_here]
    panel_mass = masses[genes_here:]
    all_rows = rows_here * lax.axis_size(CELL)
    scale = 1.0 / math.sqrt(all_rows * panel_size)
    mass_scale = 1.0 / (all_rows * panel_size)
    feature_cross = (
        jnp.dot(reduced, panel_rows, preferred_element_type=jnp.float32) * scale
    ).astype(jnp.bfloat16)
    gene_term = gene_sum * mass_scale
    peak_term = (
        jnp.dot(
            panel_mass, jnp.square(panel_rows.astype(jnp.float32)), precision=lax.Precision.HIGHEST
        )
        * mass_scale
    )
    return (feature_cross, gene_term, peak_term)


def solution(mesh):
    split = Mesh(mesh.devices.reshape(4, 4, 2, 4, 4), CELL + FEAT)
    placed = (
        P(CELL, FEAT),
        P(CELL, None),
        P(CELL),
        P(FEAT, CELL),
        P(FEAT, None),
        P(FEAT),
        P(FEAT),
    )
    return jax.shard_map(
        local,
        mesh=split,
        in_specs=placed,
        out_specs=(P(FEAT, CELL), P(FEAT), P(CELL)),
        check_vma=False,
    )
```

```python
import math

import jax
import jax.numpy as jnp
from jax import lax
from jax.sharding import Mesh
from jax.sharding import PartitionSpec as P

CELL = ("z_lo", "x", "core")
FEAT = ("z_hi", "y")
SIZES = {"z_lo": 4, "x": 4, "core": 2, "z_hi": 4, "y": 4}
STAGES = (("core", 2), ("x", 4), ("z_lo", 4))


def _shift(value, axis, size, k):
    return lax.ppermute(value, axis, [(j, (j + k) % size) for j in range(size)])


def _scatter_sum(piece, axis, size):
    index = lax.axis_index(axis)
    chunks = piece.reshape(size, piece.shape[0] // size, *piece.shape[1:])
    acc = lax.dynamic_index_in_dim(chunks, index, keepdims=False)
    for k in range(1, size):
        send = lax.dynamic_index_in_dim(chunks, (index + k) % size, keepdims=False)
        acc = acc + _shift(send, axis, size, k)
    return acc


def _gather(piece, axis, size):
    index = lax.axis_index(axis)
    out = jnp.zeros((size,) + piece.shape, piece.dtype)
    out = lax.dynamic_update_index_in_dim(out, piece, index, 0)
    for k in range(1, size):
        got = _shift(piece, axis, size, k)
        out = lax.dynamic_update_index_in_dim(out, got, (index - k) % size, 0)
    return out.reshape(size * piece.shape[0], *piece.shape[1:])


def cell_sum(total, masses):
    parts = 1
    for axis, size in STAGES:
        parts *= size
    genes, panel = total.shape
    packed = jnp.concatenate(
        [total.reshape(parts, -1), masses.reshape(parts, -1)], axis=1
    )
    for axis, size in STAGES:
        packed = _scatter_sum(packed, axis, size)
    for axis, size in reversed(STAGES):
        packed = _gather(packed, axis, size)
    cut = total.size // parts
    reduced = packed[:, :cut].reshape(genes, panel).astype(jnp.bfloat16)
    return reduced, packed[:, cut:].reshape(-1)


def local(rna_counts, rna_embed, rna_potential, atac_counts, atac_embed, atac_potential, panel_ids):
    owner = lax.axis_index(FEAT)
    local_ids = panel_ids - owner * atac_counts.shape[0]
    chosen_rows = jnp.take(atac_counts, local_ids, axis=0)
    chosen_embed = jnp.take(atac_embed, local_ids, axis=0)
    chosen_potential = jnp.take(atac_potential, local_ids, axis=0)
    small = jnp.concatenate([chosen_embed, chosen_potential[:, None]], axis=1)
    small = lax.all_gather(small, "y", axis=0, tiled=True)
    small = lax.all_gather(small, "z_hi", axis=0, tiled=True)
    panel_embed = small[:, :-1]
    panel_float = small[:, -1].astype(jnp.float32)
    panel_rows = lax.all_gather(chosen_rows, FEAT, axis=0, tiled=True)
    inverse = 1.0 / math.sqrt(rna_embed.shape[1])
    rows_here = rna_counts.shape[0]
    genes_here = rna_counts.shape[1]
    panel_size = panel_embed.shape[0]
    height = min(512, rows_here)
    number = rows_here // height
    items = (
        rna_counts.reshape(number, height, genes_here),
        rna_embed.reshape(number, height, rna_embed.shape[1]),
        rna_potential.reshape(number, height),
    )

    def advance(carry, item):
        total, gene_sum, panel_mass = carry
        block_rows, block_embed, block_potential = item
        score = lax.dot_general(
            block_embed, panel_embed, (((1,), (1,)), ((), ())), preferred_element_type=jnp.float32
        )
        coupling = jnp.exp(
            block_potential[:, None] + panel_float[None, :] + score * inverse
        ).astype(jnp.bfloat16)
        widened = coupling.astype(jnp.float32)
        row_mass = jnp.sum(widened, axis=1)
        panel_mass = panel_mass + jnp.sum(widened, axis=0)
        total = total + lax.dot_general(
            block_rows, coupling, (((0,), (0,)), ((), ())), preferred_element_type=jnp.float32
        )
        squares = jnp.square(block_rows.astype(jnp.float32))
        gene_sum = gene_sum + jnp.dot(row_mass, squares, precision=lax.Precision.HIGHEST)
        return ((total, gene_sum, panel_mass), None)

    start = (
        jnp.zeros((genes_here, panel_size), jnp.float32),
        jnp.zeros((genes_here,), jnp.float32),
        jnp.zeros((panel_size,), jnp.float32),
    )
    (total, gene_sum, panel_mass), unused = lax.scan(advance, start, items)
    reduced, masses = cell_sum(total, jnp.concatenate([gene_sum, panel_mass]))
    gene_sum = masses[:genes_here]
    panel_mass = masses[genes_here:]
    all_rows = rows_here * lax.axis_size(CELL)
    scale = 1.0 / math.sqrt(all_rows * panel_size)
    mass_scale = 1.0 / (all_rows * panel_size)
    feature_cross = (
        jnp.dot(reduced, panel_rows, preferred_element_type=jnp.float32) * scale
    ).astype(jnp.bfloat16)
    gene_term = gene_sum * mass_scale
    peak_term = (
        jnp.dot(
            panel_mass, jnp.square(panel_rows.astype(jnp.float32)), precision=lax.Precision.HIGHEST
        )
        * mass_scale
    )
    return (feature_cross, gene_term, peak_term)


def solution(mesh):
    split = Mesh(mesh.devices.reshape(4, 4, 2, 4, 4), CELL + FEAT)
    placed = (
        P(CELL, FEAT),
        P(CELL, None),
        P(CELL),
        P(FEAT, CELL),
        P(FEAT, None),
        P(FEAT),
        P(FEAT),
    )
    return jax.shard_map(
        local,
        mesh=split,
        in_specs=placed,
        out_specs=(P(FEAT, CELL), P(FEAT), P(CELL)),
        check_vma=False,
    )
```

```python
import math

import jax
import jax.numpy as jnp
from jax import lax
from jax.sharding import Mesh
from jax.sharding import PartitionSpec as P

CELL = ("z_lo", "x", "core")
FEAT = ("z_hi", "y")
SIZES = {"z_lo": 4, "x": 4, "core": 2, "z_hi": 4, "y": 4}
STAGES = (("core", 2), ("x", 4), ("z_lo", 4))


def _shift(value, axis, size, k):
    return lax.ppermute(value, axis, [(j, (j + k) % size) for j in range(size)])


def _scatter_sum(piece, axis, size):
    index = lax.axis_index(axis)
    chunks = piece.reshape(size, piece.shape[0] // size, *piece.shape[1:])
    acc = lax.dynamic_index_in_dim(chunks, index, keepdims=False)
    for k in range(1, size):
        send = lax.dynamic_index_in_dim(chunks, (index + k) % size, keepdims=False)
        acc = acc + _shift(send, axis, size, k)
    return acc


def _gather(piece, axis, size):
    index = lax.axis_index(axis)
    out = jnp.zeros((size,) + piece.shape, piece.dtype)
    out = lax.dynamic_update_index_in_dim(out, piece, index, 0)
    for k in range(1, size):
        got = _shift(piece, axis, size, k)
        out = lax.dynamic_update_index_in_dim(out, got, (index - k) % size, 0)
    return out.reshape(size * piece.shape[0], *piece.shape[1:])


def cell_sum(total, masses):
    parts = 1
    for axis, size in STAGES:
        parts *= size
    genes, panel = total.shape
    packed = jnp.concatenate(
        [total.reshape(parts, -1), masses.reshape(parts, -1)], axis=1
    )
    for axis, size in STAGES:
        packed = _scatter_sum(packed, axis, size)
    for axis, size in reversed(STAGES):
        packed = _gather(packed, axis, size)
    cut = total.size // parts
    reduced = packed[:, :cut].reshape(genes, panel).astype(jnp.bfloat16)
    return reduced, packed[:, cut:].reshape(-1)


def local(rna_counts, rna_embed, rna_potential, atac_counts, atac_embed, atac_potential, panel_ids):
    owner = lax.axis_index(FEAT)
    local_ids = panel_ids - owner * atac_counts.shape[0]
    chosen_rows = jnp.take(atac_counts, local_ids, axis=0)
    chosen_embed = jnp.take(atac_embed, local_ids, axis=0)
    chosen_potential = jnp.take(atac_potential, local_ids, axis=0)
    small = jnp.concatenate([chosen_embed, chosen_potential[:, None]], axis=1)
    small = lax.all_gather(small, "y", axis=0, tiled=True)
    small = _gather(small, "z_hi", SIZES["z_hi"])
    panel_embed = small[:, :-1]
    panel_float = small[:, -1].astype(jnp.float32)
    panel_rows = lax.all_gather(chosen_rows, FEAT, axis=0, tiled=True)
    inverse = 1.0 / math.sqrt(rna_embed.shape[1])
    rows_here = rna_counts.shape[0]
    genes_here = rna_counts.shape[1]
    panel_size = panel_embed.shape[0]
    height = min(512, rows_here)
    number = rows_here // height
    items = (
        rna_counts.reshape(number, height, genes_here),
        rna_embed.reshape(number, height, rna_embed.shape[1]),
        rna_potential.reshape(number, height),
    )

    def advance(carry, item):
        total, gene_sum, panel_mass = carry
        block_rows, block_embed, block_potential = item
        score = lax.dot_general(
            block_embed, panel_embed, (((1,), (1,)), ((), ())), preferred_element_type=jnp.float32
        )
        coupling = jnp.exp(
            block_potential[:, None] + panel_float[None, :] + score * inverse
        ).astype(jnp.bfloat16)
        widened = coupling.astype(jnp.float32)
        row_mass = jnp.sum(widened, axis=1)
        panel_mass = panel_mass + jnp.sum(widened, axis=0)
        total = total + lax.dot_general(
            block_rows, coupling, (((0,), (0,)), ((), ())), preferred_element_type=jnp.float32
        )
        squares = jnp.square(block_rows.astype(jnp.float32))
        gene_sum = gene_sum + jnp.dot(row_mass, squares, precision=lax.Precision.HIGHEST)
        return ((total, gene_sum, panel_mass), None)

    start = (
        jnp.zeros((genes_here, panel_size), jnp.float32),
        jnp.zeros((genes_here,), jnp.float32),
        jnp.zeros((panel_size,), jnp.float32),
    )
    (total, gene_sum, panel_mass), unused = lax.scan(advance, start, items)
    reduced, masses = cell_sum(total, jnp.concatenate([gene_sum, panel_mass]))
    gene_sum = masses[:genes_here]
    panel_mass = masses[genes_here:]
    all_rows = rows_here * lax.axis_size(CELL)
    scale = 1.0 / math.sqrt(all_rows * panel_size)
    mass_scale = 1.0 / (all_rows * panel_size)
    feature_cross = (
        jnp.dot(reduced, panel_rows, preferred_element_type=jnp.float32) * scale
    ).astype(jnp.bfloat16)
    gene_term = gene_sum * mass_scale
    peak_term = (
        jnp.dot(
            panel_mass, jnp.square(panel_rows.astype(jnp.float32)), precision=lax.Precision.HIGHEST
        )
        * mass_scale
    )
    return (feature_cross, gene_term, peak_term)


def solution(mesh):
    split = Mesh(mesh.devices.reshape(4, 4, 2, 4, 4), CELL + FEAT)
    placed = (
        P(CELL, FEAT),
        P(CELL, None),
        P(CELL),
        P(FEAT, CELL),
        P(FEAT, None),
        P(FEAT),
        P(FEAT),
    )
    return jax.shard_map(
        local,
        mesh=split,
        in_specs=placed,
        out_specs=(P(FEAT, CELL), P(FEAT), P(CELL)),
        check_vma=False,
    )
```

```python
import math

import jax
import jax.numpy as jnp
from jax import lax
from jax.sharding import Mesh
from jax.sharding import PartitionSpec as P

CELL = ("z_lo", "x", "core")
FEAT = ("z_hi", "y")
SIZES = {"z_lo": 4, "x": 4, "core": 2, "z_hi": 4, "y": 4}
STAGES = (("core", 2), ("x", 4), ("z_lo", 4))


def _shift(value, axis, size, k):
    return lax.ppermute(value, axis, [(j, (j + k) % size) for j in range(size)])


def _scatter_sum(piece, axis, size):
    index = lax.axis_index(axis)
    chunks = piece.reshape(size, piece.shape[0] // size, *piece.shape[1:])
    acc = lax.dynamic_index_in_dim(chunks, index, keepdims=False)
    for k in range(1, size):
        send = lax.dynamic_index_in_dim(chunks, (index + k) % size, keepdims=False)
        acc = acc + _shift(send, axis, size, k)
    return acc


def _gather(piece, axis, size):
    index = lax.axis_index(axis)
    out = jnp.zeros((size,) + piece.shape, piece.dtype)
    out = lax.dynamic_update_index_in_dim(out, piece, index, 0)
    for k in range(1, size):
        got = _shift(piece, axis, size, k)
        out = lax.dynamic_update_index_in_dim(out, got, (index - k) % size, 0)
    return out.reshape(size * piece.shape[0], *piece.shape[1:])


def cell_sum(total, masses):
    parts = 1
    for axis, size in STAGES:
        parts *= size
    genes, panel = total.shape
    packed = jnp.concatenate(
        [total.reshape(parts, -1), masses.reshape(parts, -1)], axis=1
    )
    for axis, size in STAGES:
        packed = _scatter_sum(packed, axis, size)
    packed = packed.astype(jnp.bfloat16)
    for axis, size in reversed(STAGES):
        packed = _gather(packed, axis, size)
    cut = total.size // parts
    reduced = packed[:, :cut].reshape(genes, panel)
    return reduced, packed[:, cut:].reshape(-1).astype(jnp.float32)


def local(rna_counts, rna_embed, rna_potential, atac_counts, atac_embed, atac_potential, panel_ids):
    owner = lax.axis_index(FEAT)
    local_ids = panel_ids - owner * atac_counts.shape[0]
    chosen_rows = jnp.take(atac_counts, local_ids, axis=0)
    chosen_embed = jnp.take(atac_embed, local_ids, axis=0)
    chosen_potential = jnp.take(atac_potential, local_ids, axis=0)
    small = jnp.concatenate([chosen_embed, chosen_potential[:, None]], axis=1)
    small = lax.all_gather(small, "y", axis=0, tiled=True)
    small = lax.all_gather(small, "z_hi", axis=0, tiled=True)
    panel_embed = small[:, :-1]
    panel_float = small[:, -1].astype(jnp.float32)
    panel_rows = lax.all_gather(chosen_rows, FEAT, axis=0, tiled=True)
    inverse = 1.0 / math.sqrt(rna_embed.shape[1])
    rows_here = rna_counts.shape[0]
    genes_here = rna_counts.shape[1]
    panel_size = panel_embed.shape[0]
    height = min(512, rows_here)
    number = rows_here // height
    items = (
        rna_counts.reshape(number, height, genes_here),
        rna_embed.reshape(number, height, rna_embed.shape[1]),
        rna_potential.reshape(number, height),
    )

    def advance(carry, item):
        total, gene_sum, panel_mass = carry
        block_rows, block_embed, block_potential = item
        score = lax.dot_general(
            block_embed, panel_embed, (((1,), (1,)), ((), ())), preferred_element_type=jnp.float32
        )
        coupling = jnp.exp(
            block_potential[:, None] + panel_float[None, :] + score * inverse
        ).astype(jnp.bfloat16)
        widened = coupling.astype(jnp.float32)
        row_mass = jnp.sum(widened, axis=1)
        panel_mass = panel_mass + jnp.sum(widened, axis=0)
        total = total + lax.dot_general(
            block_rows, coupling, (((0,), (0,)), ((), ())), preferred_element_type=jnp.float32
        )
        squares = jnp.square(block_rows.astype(jnp.float32))
        gene_sum = gene_sum + jnp.dot(row_mass, squares, precision=lax.Precision.HIGHEST)
        return ((total, gene_sum, panel_mass), None)

    start = (
        jnp.zeros((genes_here, panel_size), jnp.float32),
        jnp.zeros((genes_here,), jnp.float32),
        jnp.zeros((panel_size,), jnp.float32),
    )
    (total, gene_sum, panel_mass), unused = lax.scan(advance, start, items)
    reduced, masses = cell_sum(total, jnp.concatenate([gene_sum, panel_mass]))
    gene_sum = masses[:genes_here]
    panel_mass = masses[genes_here:]
    all_rows = rows_here * lax.axis_size(CELL)
    scale = 1.0 / math.sqrt(all_rows * panel_size)
    mass_scale = 1.0 / (all_rows * panel_size)
    feature_cross = (
        jnp.dot(reduced, panel_rows, preferred_element_type=jnp.float32) * scale
    ).astype(jnp.bfloat16)
    gene_term = gene_sum * mass_scale
    peak_term = (
        jnp.dot(
            panel_mass, jnp.square(panel_rows.astype(jnp.float32)), precision=lax.Precision.HIGHEST
        )
        * mass_scale
    )
    return (feature_cross, gene_term, peak_term)


def solution(mesh):
    split = Mesh(mesh.devices.reshape(4, 4, 2, 4, 4), CELL + FEAT)
    placed = (
        P(CELL, FEAT),
        P(CELL, None),
        P(CELL),
        P(FEAT, CELL),
        P(FEAT, None),
        P(FEAT),
        P(FEAT),
    )
    return jax.shard_map(
        local,
        mesh=split,
        in_specs=placed,
        out_specs=(P(FEAT, CELL), P(FEAT), P(CELL)),
        check_vma=False,
    )
```

```python
import math

import jax
import jax.numpy as jnp
from jax import lax
from jax.sharding import Mesh
from jax.sharding import PartitionSpec as P

CELL = ("z_lo", "x", "core")
FEAT = ("z_hi", "y")
SIZES = {"z_lo": 4, "x": 4, "core": 2, "z_hi": 4, "y": 4}
STAGES = (("core", 2), ("x", 4), ("z_lo", 4))


def _shift(value, axis, size, k):
    return lax.ppermute(value, axis, [(j, (j + k) % size) for j in range(size)])


def _scatter_sum(piece, axis, size):
    index = lax.axis_index(axis)
    chunks = piece.reshape(size, piece.shape[0] // size, *piece.shape[1:])
    acc = lax.dynamic_index_in_dim(chunks, index, keepdims=False)
    for k in range(1, size):
        send = lax.dynamic_index_in_dim(chunks, (index + k) % size, keepdims=False)
        acc = acc + _shift(send, axis, size, k)
    return acc


def _gather(piece, axis, size):
    index = lax.axis_index(axis)
    out = jnp.zeros((size,) + piece.shape, piece.dtype)
    out = lax.dynamic_update_index_in_dim(out, piece, index, 0)
    for k in range(1, size):
        got = _shift(piece, axis, size, k)
        out = lax.dynamic_update_index_in_dim(out, got, (index - k) % size, 0)
    return out.reshape(size * piece.shape[0], *piece.shape[1:])


def cell_sum(total, masses):
    parts = 1
    for axis, size in STAGES:
        parts *= size
    genes, panel = total.shape
    packed = jnp.concatenate(
        [total.reshape(parts, -1), masses.reshape(parts, -1)], axis=1
    )
    for axis, size in STAGES:
        packed = _scatter_sum(packed, axis, size)
    for axis, size in reversed(STAGES):
        packed = _gather(packed, axis, size)
    cut = total.size // parts
    reduced = packed[:, :cut].reshape(genes, panel).astype(jnp.bfloat16)
    return reduced, packed[:, cut:].reshape(-1)


def local(rna_counts, rna_embed, rna_potential, atac_counts, atac_embed, atac_potential, panel_ids):
    owner = lax.axis_index(FEAT)
    local_ids = panel_ids - owner * atac_counts.shape[0]
    chosen_rows = jnp.take(atac_counts, local_ids, axis=0)
    chosen_embed = jnp.take(atac_embed, local_ids, axis=0)
    chosen_potential = jnp.take(atac_potential, local_ids, axis=0)
    small = jnp.concatenate([chosen_embed, chosen_potential[:, None]], axis=1)
    small = lax.all_gather(small, "y", axis=0, tiled=True)
    small = lax.all_gather(small, "z_hi", axis=0, tiled=True)
    panel_embed = small[:, :-1]
    panel_float = small[:, -1].astype(jnp.float32)
    panel_rows = lax.all_gather(chosen_rows, FEAT, axis=0, tiled=True)
    inverse = 1.0 / math.sqrt(rna_embed.shape[1])
    rows_here = rna_counts.shape[0]
    genes_here = rna_counts.shape[1]
    panel_size = panel_embed.shape[0]
    height = min(512, rows_here)
    number = rows_here // height
    items = (
        rna_counts.reshape(number, height, genes_here),
        rna_embed.reshape(number, height, rna_embed.shape[1]),
        rna_potential.reshape(number, height),
    )

    def advance(carry, item):
        total, gene_sum, panel_mass = carry
        block_rows, block_embed, block_potential = item
        score = lax.dot_general(
            block_embed, panel_embed, (((1,), (1,)), ((), ())), preferred_element_type=jnp.float32
        )
        coupling = jnp.exp(
            block_potential[:, None] + panel_float[None, :] + score * inverse
        ).astype(jnp.bfloat16)
        widened = coupling.astype(jnp.float32)
        row_mass = jnp.sum(widened, axis=1)
        panel_mass = panel_mass + jnp.sum(widened, axis=0)
        total = total + lax.dot_general(
            block_rows, coupling, (((0,), (0,)), ((), ())), preferred_element_type=jnp.float32
        )
        squares = jnp.square(block_rows.astype(jnp.float32))
        gene_sum = gene_sum + jnp.sum(row_mass[:, None] * squares, axis=0)
        return ((total, gene_sum, panel_mass), None)

    start = (
        jnp.zeros((genes_here, panel_size), jnp.float32),
        jnp.zeros((genes_here,), jnp.float32),
        jnp.zeros((panel_size,), jnp.float32),
    )
    (total, gene_sum, panel_mass), unused = lax.scan(advance, start, items)
    reduced, masses = cell_sum(total, jnp.concatenate([gene_sum, panel_mass]))
    gene_sum = masses[:genes_here]
    panel_mass = masses[genes_here:]
    all_rows = rows_here * lax.axis_size(CELL)
    scale = 1.0 / math.sqrt(all_rows * panel_size)
    mass_scale = 1.0 / (all_rows * panel_size)
    feature_cross = (
        jnp.dot(reduced, panel_rows, preferred_element_type=jnp.float32) * scale
    ).astype(jnp.bfloat16)
    gene_term = gene_sum * mass_scale
    peak_term = (
        jnp.sum(panel_mass[:, None] * jnp.square(panel_rows.astype(jnp.float32)), axis=0)
        * mass_scale
    )
    return (feature_cross, gene_term, peak_term)


def solution(mesh):
    split = Mesh(mesh.devices.reshape(4, 4, 2, 4, 4), CELL + FEAT)
    placed = (
        P(CELL, FEAT),
        P(CELL, None),
        P(CELL),
        P(FEAT, CELL),
        P(FEAT, None),
        P(FEAT),
        P(FEAT),
    )
    return jax.shard_map(
        local,
        mesh=split,
        in_specs=placed,
        out_specs=(P(FEAT, CELL), P(FEAT), P(CELL)),
        check_vma=False,
    )
```

```python
import math

import jax
import jax.numpy as jnp
from jax import lax
from jax.sharding import Mesh
from jax.sharding import PartitionSpec as P

CELL = ("z_lo", "x", "core")
FEAT = ("z_hi", "y")
SIZES = {"z_lo": 4, "x": 4, "core": 2, "z_hi": 4, "y": 4}
STAGES = (("core", 2), ("x", 4), ("z_lo", 4))


def _shift(value, axis, size, k):
    return lax.ppermute(value, axis, [(j, (j + k) % size) for j in range(size)])


def _scatter_sum(piece, axis, size):
    index = lax.axis_index(axis)
    chunks = piece.reshape(size, piece.shape[0] // size, *piece.shape[1:])
    acc = lax.dynamic_index_in_dim(chunks, index, keepdims=False)
    for k in range(1, size):
        send = lax.dynamic_index_in_dim(chunks, (index + k) % size, keepdims=False)
        acc = acc + _shift(send, axis, size, k)
    return acc


def _gather(piece, axis, size):
    index = lax.axis_index(axis)
    out = jnp.zeros((size,) + piece.shape, piece.dtype)
    out = lax.dynamic_update_index_in_dim(out, piece, index, 0)
    for k in range(1, size):
        got = _shift(piece, axis, size, k)
        out = lax.dynamic_update_index_in_dim(out, got, (index - k) % size, 0)
    return out.reshape(size * piece.shape[0], *piece.shape[1:])


def cell_sum(total, masses):
    parts = 1
    for axis, size in STAGES:
        parts *= size
    genes, panel = total.shape
    packed = jnp.concatenate(
        [total.reshape(parts, -1), masses.reshape(parts, -1)], axis=1
    )
    for axis, size in STAGES:
        packed = _scatter_sum(packed, axis, size)
    packed = packed.astype(jnp.bfloat16)
    for axis, size in reversed(STAGES):
        packed = _gather(packed, axis, size)
    cut = total.size // parts
    reduced = packed[:, :cut].reshape(genes, panel)
    return reduced, packed[:, cut:].reshape(-1).astype(jnp.float32)


def local(rna_counts, rna_embed, rna_potential, atac_counts, atac_embed, atac_potential, panel_ids):
    owner = lax.axis_index(FEAT)
    local_ids = panel_ids - owner * atac_counts.shape[0]
    chosen_rows = jnp.take(atac_counts, local_ids, axis=0)
    chosen_embed = jnp.take(atac_embed, local_ids, axis=0)
    chosen_potential = jnp.take(atac_potential, local_ids, axis=0)
    small = jnp.concatenate([chosen_embed, chosen_potential[:, None]], axis=1)
    small = lax.all_gather(small, "y", axis=0, tiled=True)
    small = lax.all_gather(small, "z_hi", axis=0, tiled=True)
    panel_embed = small[:, :-1]
    panel_float = small[:, -1].astype(jnp.float32)
    panel_rows = lax.all_gather(chosen_rows, FEAT, axis=0, tiled=True)
    inverse = 1.0 / math.sqrt(rna_embed.shape[1])
    rows_here = rna_counts.shape[0]
    genes_here = rna_counts.shape[1]
    panel_size = panel_embed.shape[0]
    height = min(512, rows_here)
    number = rows_here // height
    items = (
        rna_counts.reshape(number, height, genes_here),
        rna_embed.reshape(number, height, rna_embed.shape[1]),
        rna_potential.reshape(number, height),
    )

    def advance(carry, item):
        total, gene_sum, panel_mass = carry
        block_rows, block_embed, block_potential = item
        score = lax.dot_general(
            block_embed, panel_embed, (((1,), (1,)), ((), ())), preferred_element_type=jnp.float32
        )
        coupling = jnp.exp(
            block_potential[:, None] + panel_float[None, :] + score * inverse
        ).astype(jnp.bfloat16)
        widened = coupling.astype(jnp.float32)
        row_mass = jnp.sum(widened, axis=1)
        panel_mass = panel_mass + jnp.sum(widened, axis=0)
        total = total + lax.dot_general(
            block_rows, coupling, (((0,), (0,)), ((), ())), preferred_element_type=jnp.float32
        )
        squares = jnp.square(block_rows.astype(jnp.float32))
        gene_sum = gene_sum + jnp.sum(row_mass[:, None] * squares, axis=0)
        return ((total, gene_sum, panel_mass), None)

    start = (
        jnp.zeros((genes_here, panel_size), jnp.float32),
        jnp.zeros((genes_here,), jnp.float32),
        jnp.zeros((panel_size,), jnp.float32),
    )
    (total, gene_sum, panel_mass), unused = lax.scan(advance, start, items)
    reduced, masses = cell_sum(total, jnp.concatenate([gene_sum, panel_mass]))
    gene_sum = masses[:genes_here]
    panel_mass = masses[genes_here:]
    all_rows = rows_here * lax.axis_size(CELL)
    scale = 1.0 / math.sqrt(all_rows * panel_size)
    mass_scale = 1.0 / (all_rows * panel_size)
    feature_cross = (
        jnp.dot(reduced, panel_rows, preferred_element_type=jnp.float32) * scale
    ).astype(jnp.bfloat16)
    gene_term = gene_sum * mass_scale
    peak_term = (
        jnp.sum(panel_mass[:, None] * jnp.square(panel_rows.astype(jnp.float32)), axis=0)
        * mass_scale
    )
    return (feature_cross, gene_term, peak_term)


def solution(mesh):
    split = Mesh(mesh.devices.reshape(4, 4, 2, 4, 4), CELL + FEAT)
    placed = (
        P(CELL, FEAT),
        P(CELL, None),
        P(CELL),
        P(FEAT, CELL),
        P(FEAT, None),
        P(FEAT),
        P(FEAT),
    )
    return jax.shard_map(
        local,
        mesh=split,
        in_specs=placed,
        out_specs=(P(FEAT, CELL), P(FEAT), P(CELL)),
        check_vma=False,
    )
```

```python
import math

import jax
import jax.numpy as jnp
from jax import lax
from jax.sharding import Mesh
from jax.sharding import PartitionSpec as P

CELL = ("z_lo", "x", "core")
FEAT = ("z_hi", "y")
SIZES = {"z_lo": 4, "x": 4, "core": 2, "z_hi": 4, "y": 4}
STAGES = (("core", 2), ("x", 4), ("z_lo", 4))


def _shift(value, axis, size, k):
    return lax.ppermute(value, axis, [(j, (j + k) % size) for j in range(size)])


def _scatter_sum(piece, axis, size):
    index = lax.axis_index(axis)
    chunks = piece.reshape(size, piece.shape[0] // size, *piece.shape[1:])
    acc = lax.dynamic_index_in_dim(chunks, index, keepdims=False)
    for k in range(1, size):
        send = lax.dynamic_index_in_dim(chunks, (index + k) % size, keepdims=False)
        acc = acc + _shift(send, axis, size, k)
    return acc


def _gather(piece, axis, size):
    index = lax.axis_index(axis)
    out = jnp.zeros((size,) + piece.shape, piece.dtype)
    out = lax.dynamic_update_index_in_dim(out, piece, index, 0)
    for k in range(1, size):
        got = _shift(piece, axis, size, k)
        out = lax.dynamic_update_index_in_dim(out, got, (index - k) % size, 0)
    return out.reshape(size * piece.shape[0], *piece.shape[1:])


def cell_sum(total, masses):
    parts = 1
    for axis, size in STAGES:
        parts *= size
    genes, panel = total.shape
    packed = jnp.concatenate(
        [total.reshape(parts, -1), masses.reshape(parts, -1)], axis=1
    )
    for axis, size in STAGES:
        packed = _scatter_sum(packed, axis, size)
    packed = packed.astype(jnp.bfloat16)
    for axis, size in reversed(STAGES):
        packed = _gather(packed, axis, size)
    cut = total.size // parts
    reduced = packed[:, :cut].reshape(genes, panel)
    return reduced, packed[:, cut:].reshape(-1).astype(jnp.float32)


def local(rna_counts, rna_embed, rna_potential, atac_counts, atac_embed, atac_potential, panel_ids):
    owner = lax.axis_index(FEAT)
    local_ids = panel_ids - owner * atac_counts.shape[0]
    chosen_rows = jnp.take(atac_counts, local_ids, axis=0)
    chosen_embed = jnp.take(atac_embed, local_ids, axis=0)
    chosen_potential = jnp.take(atac_potential, local_ids, axis=0)
    small = jnp.concatenate([chosen_embed, chosen_potential[:, None]], axis=1)
    small = lax.all_gather(small, "y", axis=0, tiled=True)
    small = lax.all_gather(small, "z_hi", axis=0, tiled=True)
    panel_embed = small[:, :-1]
    panel_float = small[:, -1].astype(jnp.float32)
    panel_rows = lax.all_gather(chosen_rows, FEAT, axis=0, tiled=True)
    inverse = 1.0 / math.sqrt(rna_embed.shape[1])
    rows_here = rna_counts.shape[0]
    genes_here = rna_counts.shape[1]
    panel_size = panel_embed.shape[0]
    height = min(1024, rows_here)
    number = rows_here // height
    items = (
        rna_counts.reshape(number, height, genes_here),
        rna_embed.reshape(number, height, rna_embed.shape[1]),
        rna_potential.reshape(number, height),
    )

    def advance(carry, item):
        total, gene_sum, panel_mass = carry
        block_rows, block_embed, block_potential = item
        score = lax.dot_general(
            block_embed, panel_embed, (((1,), (1,)), ((), ())), preferred_element_type=jnp.float32
        )
        coupling = jnp.exp(
            block_potential[:, None] + panel_float[None, :] + score * inverse
        ).astype(jnp.bfloat16)
        widened = coupling.astype(jnp.float32)
        row_mass = jnp.sum(widened, axis=1)
        panel_mass = panel_mass + jnp.sum(widened, axis=0)
        total = total + lax.dot_general(
            block_rows, coupling, (((0,), (0,)), ((), ())), preferred_element_type=jnp.float32
        )
        squares = jnp.square(block_rows.astype(jnp.float32))
        gene_sum = gene_sum + jnp.sum(row_mass[:, None] * squares, axis=0)
        return ((total, gene_sum, panel_mass), None)

    start = (
        jnp.zeros((genes_here, panel_size), jnp.float32),
        jnp.zeros((genes_here,), jnp.float32),
        jnp.zeros((panel_size,), jnp.float32),
    )
    (total, gene_sum, panel_mass), unused = lax.scan(advance, start, items)
    reduced, masses = cell_sum(total, jnp.concatenate([gene_sum, panel_mass]))
    gene_sum = masses[:genes_here]
    panel_mass = masses[genes_here:]
    all_rows = rows_here * lax.axis_size(CELL)
    scale = 1.0 / math.sqrt(all_rows * panel_size)
    mass_scale = 1.0 / (all_rows * panel_size)
    feature_cross = (
        jnp.dot(reduced, panel_rows, preferred_element_type=jnp.float32) * scale
    ).astype(jnp.bfloat16)
    gene_term = gene_sum * mass_scale
    peak_term = (
        jnp.sum(panel_mass[:, None] * jnp.square(panel_rows.astype(jnp.float32)), axis=0)
        * mass_scale
    )
    return (feature_cross, gene_term, peak_term)


def solution(mesh):
    split = Mesh(mesh.devices.reshape(4, 4, 2, 4, 4), CELL + FEAT)
    placed = (
        P(CELL, FEAT),
        P(CELL, None),
        P(CELL),
        P(FEAT, CELL),
        P(FEAT, None),
        P(FEAT),
        P(FEAT),
    )
    return jax.shard_map(
        local,
        mesh=split,
        in_specs=placed,
        out_specs=(P(FEAT, CELL), P(FEAT), P(CELL)),
        check_vma=False,
    )
```

```python
import math

import jax
import jax.numpy as jnp
from jax import lax
from jax.sharding import Mesh
from jax.sharding import PartitionSpec as P

CELL = ("z_lo", "x", "core")
FEAT = ("z_hi", "y")
SIZES = {"z_lo": 4, "x": 4, "core": 2, "z_hi": 4, "y": 4}
STAGES = (("core", 2), ("x", 4), ("z_lo", 4))


def _shift(value, axis, size, k):
    return lax.ppermute(value, axis, [(j, (j + k) % size) for j in range(size)])


def _scatter_sum(piece, axis, size):
    index = lax.axis_index(axis)
    chunks = piece.reshape(size, piece.shape[0] // size, *piece.shape[1:])
    acc = lax.dynamic_index_in_dim(chunks, index, keepdims=False)
    for k in range(1, size):
        send = lax.dynamic_index_in_dim(chunks, (index + k) % size, keepdims=False)
        acc = acc + _shift(send, axis, size, k)
    return acc


def _gather(piece, axis, size):
    index = lax.axis_index(axis)
    out = jnp.zeros((size,) + piece.shape, piece.dtype)
    out = lax.dynamic_update_index_in_dim(out, piece, index, 0)
    for k in range(1, size):
        got = _shift(piece, axis, size, k)
        out = lax.dynamic_update_index_in_dim(out, got, (index - k) % size, 0)
    return out.reshape(size * piece.shape[0], *piece.shape[1:])


def cell_sum(total, masses):
    parts = 1
    for axis, size in STAGES:
        parts *= size
    genes, panel = total.shape
    packed = jnp.concatenate(
        [total.reshape(parts, -1), masses.reshape(parts, -1)], axis=1
    )
    for axis, size in STAGES:
        packed = _scatter_sum(packed, axis, size)
    packed = packed.astype(jnp.bfloat16)
    for axis, size in reversed(STAGES):
        packed = _gather(packed, axis, size)
    cut = total.size // parts
    reduced = packed[:, :cut].reshape(genes, panel)
    return reduced, packed[:, cut:].reshape(-1).astype(jnp.float32)


def local(rna_counts, rna_embed, rna_potential, atac_counts, atac_embed, atac_potential, panel_ids):
    owner = lax.axis_index(FEAT)
    local_ids = panel_ids - owner * atac_counts.shape[0]
    chosen_rows = jnp.take(atac_counts, local_ids, axis=0)
    chosen_embed = jnp.take(atac_embed, local_ids, axis=0)
    chosen_potential = jnp.take(atac_potential, local_ids, axis=0)
    small = jnp.concatenate([chosen_embed, chosen_potential[:, None]], axis=1)
    small = lax.all_gather(small, "y", axis=0, tiled=True)
    small = lax.all_gather(small, "z_hi", axis=0, tiled=True)
    panel_embed = small[:, :-1]
    panel_float = small[:, -1].astype(jnp.float32)
    panel_rows = lax.all_gather(chosen_rows, FEAT, axis=0, tiled=True)
    inverse = 1.0 / math.sqrt(rna_embed.shape[1])
    rows_here = rna_counts.shape[0]
    genes_here = rna_counts.shape[1]
    panel_size = panel_embed.shape[0]
    height = min(2048, rows_here)
    number = rows_here // height
    items = (
        rna_counts.reshape(number, height, genes_here),
        rna_embed.reshape(number, height, rna_embed.shape[1]),
        rna_potential.reshape(number, height),
    )

    def advance(carry, item):
        total, gene_sum, panel_mass = carry
        block_rows, block_embed, block_potential = item
        score = lax.dot_general(
            block_embed, panel_embed, (((1,), (1,)), ((), ())), preferred_element_type=jnp.float32
        )
        coupling = jnp.exp(
            block_potential[:, None] + panel_float[None, :] + score * inverse
        ).astype(jnp.bfloat16)
        widened = coupling.astype(jnp.float32)
        row_mass = jnp.sum(widened, axis=1)
        panel_mass = panel_mass + jnp.sum(widened, axis=0)
        total = total + lax.dot_general(
            block_rows, coupling, (((0,), (0,)), ((), ())), preferred_element_type=jnp.float32
        )
        squares = jnp.square(block_rows.astype(jnp.float32))
        gene_sum = gene_sum + jnp.sum(row_mass[:, None] * squares, axis=0)
        return ((total, gene_sum, panel_mass), None)

    start = (
        jnp.zeros((genes_here, panel_size), jnp.float32),
        jnp.zeros((genes_here,), jnp.float32),
        jnp.zeros((panel_size,), jnp.float32),
    )
    (total, gene_sum, panel_mass), unused = lax.scan(advance, start, items)
    reduced, masses = cell_sum(total, jnp.concatenate([gene_sum, panel_mass]))
    gene_sum = masses[:genes_here]
    panel_mass = masses[genes_here:]
    all_rows = rows_here * lax.axis_size(CELL)
    scale = 1.0 / math.sqrt(all_rows * panel_size)
    mass_scale = 1.0 / (all_rows * panel_size)
    feature_cross = (
        jnp.dot(reduced, panel_rows, preferred_element_type=jnp.float32) * scale
    ).astype(jnp.bfloat16)
    gene_term = gene_sum * mass_scale
    peak_term = (
        jnp.sum(panel_mass[:, None] * jnp.square(panel_rows.astype(jnp.float32)), axis=0)
        * mass_scale
    )
    return (feature_cross, gene_term, peak_term)


def solution(mesh):
    split = Mesh(mesh.devices.reshape(4, 4, 2, 4, 4), CELL + FEAT)
    placed = (
        P(CELL, FEAT),
        P(CELL, None),
        P(CELL),
        P(FEAT, CELL),
        P(FEAT, None),
        P(FEAT),
        P(FEAT),
    )
    return jax.shard_map(
        local,
        mesh=split,
        in_specs=placed,
        out_specs=(P(FEAT, CELL), P(FEAT), P(CELL)),
        check_vma=False,
    )
```

```python
import math

import jax
import jax.numpy as jnp
from jax import lax
from jax.sharding import Mesh
from jax.sharding import PartitionSpec as P

CELL = ("z_lo", "x", "core")
FEAT = ("z_hi", "y")
SIZES = {"z_lo": 4, "x": 4, "core": 2, "z_hi": 4, "y": 4}
STAGES = (("core", 2), ("x", 4), ("z_lo", 4))


def _shift(value, axis, size, k):
    return lax.ppermute(value, axis, [(j, (j + k) % size) for j in range(size)])


def _scatter_sum(piece, axis, size):
    index = lax.axis_index(axis)
    chunks = piece.reshape(size, piece.shape[0] // size, *piece.shape[1:])
    acc = lax.dynamic_index_in_dim(chunks, index, keepdims=False)
    for k in range(1, size):
        send = lax.dynamic_index_in_dim(chunks, (index + k) % size, keepdims=False)
        acc = acc + _shift(send, axis, size, k)
    return acc


def _gather(piece, axis, size):
    index = lax.axis_index(axis)
    out = jnp.zeros((size,) + piece.shape, piece.dtype)
    out = lax.dynamic_update_index_in_dim(out, piece, index, 0)
    for k in range(1, size):
        got = _shift(piece, axis, size, k)
        out = lax.dynamic_update_index_in_dim(out, got, (index - k) % size, 0)
    return out.reshape(size * piece.shape[0], *piece.shape[1:])


def cell_sum(total, masses):
    parts = 1
    for axis, size in STAGES:
        parts *= size
    genes, panel = total.shape
    packed = jnp.concatenate(
        [total.reshape(parts, -1), masses.reshape(parts, -1)], axis=1
    )
    for axis, size in STAGES:
        packed = _scatter_sum(packed, axis, size)
    packed = packed.astype(jnp.bfloat16)
    for axis, size in reversed(STAGES):
        packed = _gather(packed, axis, size)
    cut = total.size // parts
    reduced = packed[:, :cut].reshape(genes, panel)
    return reduced, packed[:, cut:].reshape(-1).astype(jnp.float32)


def local(rna_counts, rna_embed, rna_potential, atac_counts, atac_embed, atac_potential, panel_ids):
    owner = lax.axis_index(FEAT)
    local_ids = panel_ids - owner * atac_counts.shape[0]
    chosen_rows = jnp.take(atac_counts, local_ids, axis=0)
    chosen_embed = jnp.take(atac_embed, local_ids, axis=0)
    chosen_potential = jnp.take(atac_potential, local_ids, axis=0)
    small = jnp.concatenate([chosen_embed, chosen_potential[:, None]], axis=1)
    small = lax.all_gather(small, "z_hi", axis=0, tiled=True)
    small = lax.all_gather(small, "y", axis=0, tiled=False)
    small = small.reshape(SIZES["y"], SIZES["z_hi"], -1, small.shape[-1])
    small = small.transpose(1, 0, 2, 3).reshape(-1, small.shape[-1])
    panel_embed = small[:, :-1]
    panel_float = small[:, -1].astype(jnp.float32)
    panel_rows = lax.all_gather(chosen_rows, FEAT, axis=0, tiled=True)
    inverse = 1.0 / math.sqrt(rna_embed.shape[1])
    rows_here = rna_counts.shape[0]
    genes_here = rna_counts.shape[1]
    panel_size = panel_embed.shape[0]
    height = min(2048, rows_here)
    number = rows_here // height
    items = (
        rna_counts.reshape(number, height, genes_here),
        rna_embed.reshape(number, height, rna_embed.shape[1]),
        rna_potential.reshape(number, height),
    )

    def advance(carry, item):
        total, gene_sum, panel_mass = carry
        block_rows, block_embed, block_potential = item
        score = lax.dot_general(
            block_embed, panel_embed, (((1,), (1,)), ((), ())), preferred_element_type=jnp.float32
        )
        coupling = jnp.exp(
            block_potential[:, None] + panel_float[None, :] + score * inverse
        ).astype(jnp.bfloat16)
        widened = coupling.astype(jnp.float32)
        row_mass = jnp.sum(widened, axis=1)
        panel_mass = panel_mass + jnp.sum(widened, axis=0)
        total = total + lax.dot_general(
            block_rows, coupling, (((0,), (0,)), ((), ())), preferred_element_type=jnp.float32
        )
        squares = jnp.square(block_rows.astype(jnp.float32))
        gene_sum = gene_sum + jnp.sum(row_mass[:, None] * squares, axis=0)
        return ((total, gene_sum, panel_mass), None)

    start = (
        jnp.zeros((genes_here, panel_size), jnp.float32),
        jnp.zeros((genes_here,), jnp.float32),
        jnp.zeros((panel_size,), jnp.float32),
    )
    (total, gene_sum, panel_mass), unused = lax.scan(advance, start, items)
    reduced, masses = cell_sum(total, jnp.concatenate([gene_sum, panel_mass]))
    gene_sum = masses[:genes_here]
    panel_mass = masses[genes_here:]
    all_rows = rows_here * lax.axis_size(CELL)
    scale = 1.0 / math.sqrt(all_rows * panel_size)
    mass_scale = 1.0 / (all_rows * panel_size)
    feature_cross = (
        jnp.dot(reduced, panel_rows, preferred_element_type=jnp.float32) * scale
    ).astype(jnp.bfloat16)
    gene_term = gene_sum * mass_scale
    peak_term = (
        jnp.sum(panel_mass[:, None] * jnp.square(panel_rows.astype(jnp.float32)), axis=0)
        * mass_scale
    )
    return (feature_cross, gene_term, peak_term)


def solution(mesh):
    split = Mesh(mesh.devices.reshape(4, 4, 2, 4, 4), CELL + FEAT)
    placed = (
        P(CELL, FEAT),
        P(CELL, None),
        P(CELL),
        P(FEAT, CELL),
        P(FEAT, None),
        P(FEAT),
        P(FEAT),
    )
    return jax.shard_map(
        local,
        mesh=split,
        in_specs=placed,
        out_specs=(P(FEAT, CELL), P(FEAT), P(CELL)),
        check_vma=False,
    )
```

```python
import math

import jax
import jax.numpy as jnp
from jax import lax
from jax.sharding import Mesh
from jax.sharding import PartitionSpec as P

CELL = ("z_lo", "x", "core")
FEAT = ("z_hi", "y")
SIZES = {"z_lo": 4, "x": 4, "core": 2, "z_hi": 4, "y": 4}
STAGES = (("core", 2), ("x", 4), ("z_lo", 4))


def _shift(value, axis, size, k):
    return lax.ppermute(value, axis, [(j, (j + k) % size) for j in range(size)])


def _scatter_sum(piece, axis, size):
    index = lax.axis_index(axis)
    chunks = piece.reshape(size, piece.shape[0] // size, *piece.shape[1:])
    acc = lax.dynamic_index_in_dim(chunks, index, keepdims=False)
    for k in range(1, size):
        send = lax.dynamic_index_in_dim(chunks, (index + k) % size, keepdims=False)
        acc = acc + _shift(send, axis, size, k)
    return acc


def _gather(piece, axis, size):
    index = lax.axis_index(axis)
    out = jnp.zeros((size,) + piece.shape, piece.dtype)
    out = lax.dynamic_update_index_in_dim(out, piece, index, 0)
    for k in range(1, size):
        got = _shift(piece, axis, size, k)
        out = lax.dynamic_update_index_in_dim(out, got, (index - k) % size, 0)
    return out.reshape(size * piece.shape[0], *piece.shape[1:])


def cell_sum(total, masses):
    parts = 1
    for axis, size in STAGES:
        parts *= size
    genes, panel = total.shape
    packed = jnp.concatenate(
        [total.reshape(parts, -1), masses.reshape(parts, -1)], axis=1
    )
    for axis, size in STAGES:
        packed = _scatter_sum(packed, axis, size)
    packed = packed.astype(jnp.bfloat16)
    for axis, size in reversed(STAGES):
        packed = _gather(packed, axis, size)
    cut = total.size // parts
    reduced = packed[:, :cut].reshape(genes, panel)
    return reduced, packed[:, cut:].reshape(-1).astype(jnp.float32)


def local(rna_counts, rna_embed, rna_potential, atac_counts, atac_embed, atac_potential, panel_ids):
    owner = lax.axis_index(FEAT)
    local_ids = panel_ids - owner * atac_counts.shape[0]
    chosen_rows = jnp.take(atac_counts, local_ids, axis=0)
    chosen_embed = jnp.take(atac_embed, local_ids, axis=0)
    chosen_potential = jnp.take(atac_potential, local_ids, axis=0)
    small = jnp.concatenate([chosen_embed.reshape(-1), chosen_potential])
    lanes = 128
    rows = -(-small.shape[0] // lanes)
    small = jnp.pad(small, (0, rows * lanes - small.shape[0])).reshape(rows, lanes)
    small = lax.all_gather(small, "z_hi", axis=0, tiled=True)
    small = lax.all_gather(small, "y", axis=0, tiled=False)
    small = small.reshape(SIZES["y"], SIZES["z_hi"], rows * lanes)
    small = small.transpose(1, 0, 2).reshape(SIZES["z_hi"] * SIZES["y"], -1)
    cut = chosen_embed.size
    panel_embed = small[:, :cut].reshape(-1, chosen_embed.shape[1])
    panel_float = small[:, cut:cut + chosen_potential.size].reshape(-1).astype(jnp.float32)
    panel_rows = lax.all_gather(chosen_rows, FEAT, axis=0, tiled=True)
    inverse = 1.0 / math.sqrt(rna_embed.shape[1])
    rows_here = rna_counts.shape[0]
    genes_here = rna_counts.shape[1]
    panel_size = panel_embed.shape[0]
    height = min(2048, rows_here)
    number = rows_here // height
    items = (
        rna_counts.reshape(number, height, genes_here),
        rna_embed.reshape(number, height, rna_embed.shape[1]),
        rna_potential.reshape(number, height),
    )

    def advance(carry, item):
        total, gene_sum, panel_mass = carry
        block_rows, block_embed, block_potential = item
        score = lax.dot_general(
            block_embed, panel_embed, (((1,), (1,)), ((), ())), preferred_element_type=jnp.float32
        )
        coupling = jnp.exp(
            block_potential[:, None] + panel_float[None, :] + score * inverse
        ).astype(jnp.bfloat16)
        widened = coupling.astype(jnp.float32)
        row_mass = jnp.sum(widened, axis=1)
        panel_mass = panel_mass + jnp.sum(widened, axis=0)
        total = total + lax.dot_general(
            block_rows, coupling, (((0,), (0,)), ((), ())), preferred_element_type=jnp.float32
        )
        squares = jnp.square(block_rows.astype(jnp.float32))
        gene_sum = gene_sum + jnp.sum(row_mass[:, None] * squares, axis=0)
        return ((total, gene_sum, panel_mass), None)

    start = (
        jnp.zeros((genes_here, panel_size), jnp.float32),
        jnp.zeros((genes_here,), jnp.float32),
        jnp.zeros((panel_size,), jnp.float32),
    )
    (total, gene_sum, panel_mass), unused = lax.scan(advance, start, items)
    reduced, masses = cell_sum(total, jnp.concatenate([gene_sum, panel_mass]))
    gene_sum = masses[:genes_here]
    panel_mass = masses[genes_here:]
    all_rows = rows_here * lax.axis_size(CELL)
    scale = 1.0 / math.sqrt(all_rows * panel_size)
    mass_scale = 1.0 / (all_rows * panel_size)
    feature_cross = (
        jnp.dot(reduced, panel_rows, preferred_element_type=jnp.float32) * scale
    ).astype(jnp.bfloat16)
    gene_term = gene_sum * mass_scale
    peak_term = (
        jnp.sum(panel_mass[:, None] * jnp.square(panel_rows.astype(jnp.float32)), axis=0)
        * mass_scale
    )
    return (feature_cross, gene_term, peak_term)


def solution(mesh):
    split = Mesh(mesh.devices.reshape(4, 4, 2, 4, 4), CELL + FEAT)
    placed = (
        P(CELL, FEAT),
        P(CELL, None),
        P(CELL),
        P(FEAT, CELL),
        P(FEAT, None),
        P(FEAT),
        P(FEAT),
    )
    return jax.shard_map(
        local,
        mesh=split,
        in_specs=placed,
        out_specs=(P(FEAT, CELL), P(FEAT), P(CELL)),
        check_vma=False,
    )
```
